128 devices in a mesh: grow: 8 (over x_lo, y), gcol: 16 (over z, x_hi, core).
Axes of the slice: x: 4 (x_hi: 2, x_lo: 2; x = x_hi * 2 + x_lo), y: 4, z: 4, core: 2. Of those that a mesh axis runs over, the one named last changes fastest.
Arguments:
- screened: bfloat16 [2, 16384, 16384], P(None, 'grow', 'gcol'), may hold values from -6 to 6
- elements: bfloat16 [2, 1024, 16384], P(None, None, ('grow', 'gcol')), may hold values from -0.046875 to 0.046875
- energy_grid: float32 [256], replicated, may hold values from -3 to 3
- band_index: int32 [256], replicated, may hold values from 0 to 255
- energy_index: int32 [4, 16], replicated, may hold values from 0 to 255
Outputs:
- sigma: float32 [2, 4, 16], replicated
The draws below stay inside these ranges and needn't reach their ends.
All inputs are finite; a program needn't handle non-finite values.
Results may differ from the reference program's by a relative error of at most 0.0003.
Values may be sent and summed in bfloat16 or wider, within the bound.
No kernel may reach another device: no remote copies, remote signals or barrier semaphores. Data moves between devices by JAX's collectives and lax.ppermute only.
A program may use at most 128 MiB of HBM per device.

```python
import jax
import jax.numpy as jnp
from jax import lax

NG = 16384
NSUM = 256
NB_OUT = 4
NE = 16
NGRID = 256
PAIRS = 1024


def plant(result, stream_key, smallest, top_value):
    spot = [jax.random.randint(jax.random.fold_in(stream_key, axis), (), 0, length) for axis, length in enumerate(result.shape)]
    widest = result.shape.index(max(result.shape))
    beside = spot[:widest] + [(spot[widest] + 1) % result.shape[widest]] + spot[widest + 1:]
    return result.at[tuple(spot)].set(smallest).at[tuple(beside)].set(top_value)


def shard_levels(rng, shape, split, least, high):
    def one(axis_at, blocks):
        heights = jax.random.uniform(jax.random.fold_in(jax.random.fold_in(rng, 6), axis_at), (blocks,), jnp.float32, least / len(split), high / len(split))
        return jnp.repeat(jnp.exp(heights), shape[axis_at] // blocks).reshape((-1,) + (1,) * (len(shape) - axis_at - 1))

    loudness = one(*split[0])
    for cut in split[1:]:
        loudness = loudness * one(*cut)
    return loudness


def gaussian(own_key, extent, deviation, limit, pieces=(), kind=jnp.bfloat16):
    entries = jax.random.normal(own_key, extent, jnp.float32) * deviation
    if len(pieces) > 0:
        entries = shard_levels(own_key, extent, pieces, -0.22, 0.18) * entries
    return jnp.clip(entries, min=-limit, max=limit).astype(kind)


def setup_inputs(seed: int = 0) -> dict:
    key_list = jax.random.split(jax.random.key(seed), 6)
    screened = gaussian(key_list[0], (2, NG, NG), 1.0, 6.0, ((1, 8), (2, 16)))
    elements = gaussian(key_list[1], (2, PAIRS, NG), NG ** -0.5, 0.046875, ((2, 128),))
    energy_grid = jnp.clip(jax.random.uniform(key_list[2], (NGRID,), jnp.float32, -3.0, 3.0), -3.0, 3.0)
    band_index = plant(jax.random.randint(key_list[3], (NSUM,), 0, NGRID), jax.random.fold_in(key_list[3], 1), 0, NGRID - 1).astype(jnp.int32)
    energy_index = plant(jax.random.randint(key_list[4], (NB_OUT, NE), 0, NGRID), jax.random.fold_in(key_list[4], 1), 0, NGRID - 1).astype(jnp.int32)
    return {"screened": screened, "elements": elements, "energy_grid": energy_grid, "band_index": band_index, "energy_index": energy_index}


def weights(energy_grid, band_index, energy_index):
    band_energy = jnp.take(energy_grid, band_index)
    eval_energy = jnp.take(energy_grid, energy_index)
    offset = eval_energy[:, None, :] - band_energy[None, :, None]
    denom = offset * offset + 0.25
    return offset / denom, -0.5 / denom


def reference(screened, elements, energy_grid, band_index, energy_index):
    blocks = 8
    size = NG // blocks
    mats = elements.astype(jnp.float32)

    def step(carry, block):
        wblock = lax.dynamic_slice_in_dim(screened, block * size, size, 1).astype(jnp.float32)
        mblock = lax.dynamic_slice_in_dim(mats, block * size, size, 2)
        prod = jnp.einsum("mph,wgh->mpwg", mats, wblock)
        yre = prod[0, :, 0] - prod[1, :, 1]
        yim = prod[1, :, 0] + prod[0, :, 1]
        sre = jnp.sum(mblock[0] * yre + mblock[1] * yim, axis=-1)
        sim = jnp.sum(mblock[0] * yim - mblock[1] * yre, axis=-1)
        return (carry[0] + sre, carry[1] + sim), None

    zero = jnp.zeros((PAIRS,), jnp.float32)
    (s_re, s_im), _ = lax.scan(step, (zero, zero), jnp.arange(blocks, dtype=jnp.int32))
    wre, wim = weights(energy_grid, band_index, energy_index)
    sre = s_re.reshape(NB_OUT, NSUM)[:, :, None]
    sim = s_im.reshape(NB_OUT, NSUM)[:, :, None]
    scale = NSUM ** -0.5
    out_re = scale * jnp.sum(wre * sre - wim * sim, axis=1)
    out_im = scale * jnp.sum(wre * sim + wim * sre, axis=1)
    return jnp.stack([out_re, out_im])
```

```python
import functools
import itertools

import jax
import jax.numpy as jnp
from jax import lax
from jax.experimental import pallas as pl
from jax.experimental.pallas import tpu as pltpu
from jax.sharding import Mesh
from jax.sharding import PartitionSpec as P

AXES = ("x_lo", "y", "z", "x_hi", "core")
ROW = ("x_lo", "y")
COL = ("z", "x_hi", "core")
STEP = 128
HALF = 512

MATCH = (
    (2, 0, 5, 7, 1, 3, 4, 6),
    (2, 3, 5, 4, 1, 0, 7, 6),
    (7, 4, 3, 1, 6, 5, 0, 2),
    (6, 7, 0, 2, 4, 5, 3, 1),
    (2, 0, 5, 4, 1, 3, 7, 6),
    (2, 0, 5, 4, 3, 1, 6, 7),
    (6, 4, 2, 1, 7, 5, 0, 3),
    (4, 6, 2, 0, 5, 7, 3, 1),
    (6, 4, 3, 1, 5, 7, 0, 2),
    (6, 7, 1, 0, 4, 5, 3, 2),
    (2, 0, 5, 6, 1, 3, 7, 4),
    (1, 3, 5, 4, 2, 0, 6, 7),
    (7, 6, 3, 1, 5, 4, 0, 2),
    (6, 7, 3, 1, 4, 5, 2, 0),
    (3, 0, 5, 7, 1, 2, 4, 6),
    (1, 3, 7, 5, 0, 2, 4, 6),
)


def pairs_of(move):
    found = []
    for x_lo, y, z, x_hi, core in itertools.product(range(2), range(4), range(4), range(2), range(2)):
        x, ny, nz, ncore = move(2 * x_hi + x_lo, y, z, core)
        x, ny, nz = x % 4, ny % 4, nz % 4
        source = (((x_lo * 4 + y) * 4 + z) * 2 + x_hi) * 2 + core
        found.append((source, (((x % 2 * 4 + ny) * 4 + nz) * 2 + x // 2) * 2 + ncore))
    return found


Z_UP = pairs_of(lambda x, y, z, c: (x, y, z + 1, c))
Z_DOWN = pairs_of(lambda x, y, z, c: (x, y, z - 1, c))
Z_ON = pairs_of(lambda x, y, z, c: (x, y, z + 1 - 2 * c, c))
Y_UP = pairs_of(lambda x, y, z, c: (x, y + 1, z, c))
Y_DOWN = pairs_of(lambda x, y, z, c: (x, y - 1, z, c))
Y_ON = pairs_of(lambda x, y, z, c: (x, y + 1 - 2 * c, z, c))
X_FAR = pairs_of(lambda x, y, z, c: (x + 2, y, z, c))
X_NEAR = pairs_of(lambda x, y, z, c: (x ^ 1, y, z, c))
CORE = pairs_of(lambda x, y, z, c: (x, y, z, 1 - c))
TURN = [(c // 2 * 16 + c % 2 * 8 + j, MATCH[c][j] * 16 + c) for c in range(16) for j in range(8)]
ROUNDS = (
    CORE,
    X_NEAR,
    pairs_of(lambda x, y, z, c: (x + (1 if x % 2 else -1), y, z, c)),
    pairs_of(lambda x, y, z, c: (x, y ^ 1, z, c)),
    pairs_of(lambda x, y, z, c: (x, y + (1 if y % 2 else -1), z, c)),
    pairs_of(lambda x, y, z, c: (x, y, z ^ 1, c)),
    pairs_of(lambda x, y, z, c: (x, y, z + (1 if z % 2 else -1), c)),
)


def send(block, pairs):
    return lax.ppermute(block, AXES, pairs)


def ring(block, up, down, on, core):
    below = send(block, up)
    above = send(block, down)
    far = send(jnp.where(core == 0, below, above), on)
    return [block, below, above, far]


def weights(energy_grid, band_index, energy_index):
    points = lax.broadcasted_iota(jnp.int32, (1, energy_grid.shape[0]), 1)
    band_energy = jnp.sum(
        jnp.where(band_index[:, None] == points, energy_grid[None, :], 0.0), axis=-1
    )
    eval_energy = jnp.sum(
        jnp.where(energy_index[:, :, None] == points[None], energy_grid[None, None, :], 0.0),
        axis=-1,
    )
    offset = eval_energy[:, None, :] - band_energy[None, :, None]
    denom = offset * offset + 0.25
    scale = band_index.shape[0] ** (-0.5)
    w = jnp.stack([offset / denom, -0.5 / denom]) * scale
    return w.reshape(2, -1, w.shape[-1])


def product_body(place, *refs):
    blocks, w_ref, z_ref, lhs = refs[:16], refs[16], refs[-2], refs[-1]

    @pl.when(pl.program_id(0) == 0)
    def _():
        for i, block in enumerate(blocks):
            at = pl.multiple_of(place[i] * STEP, STEP)
            late = pl.multiple_of(place[i] * STEP + 2048, STEP)
            re, im = block[0], block[1]
            lhs[:HALF, pl.ds(at, STEP)] = re
            lhs[:HALF, pl.ds(late, STEP)] = im
            lhs[HALF:, pl.ds(at, STEP)] = -im
            lhs[HALF:, pl.ds(late, STEP)] = re

    w = w_ref[...].reshape(4096, -1)
    for m in range(4):
        part = jnp.dot(lhs[m * 256 : m * 256 + 256, :], w, preferred_element_type=jnp.float32)
        z_ref[m // 2, m % 2 * 256 : m % 2 * 256 + 256, :] = part


def product(chunk, place, blocks, screened, z=None):
    width = 256
    specs = [pl.BlockSpec((2, HALF, STEP), lambda n, s: (0, chunk, 0))] * 16
    specs.append(pl.BlockSpec((2, 2048, width), lambda n, s: (0, 0, n)))
    args = [place, *blocks, screened]
    alias = {}
    if z is not None:
        specs.append(pl.BlockSpec(memory_space=pl.ANY))
        args.append(z)
        alias = {18: 0}
    return pl.pallas_call(
        product_body,
        out_shape=jax.ShapeDtypeStruct((2, 1024, 1024), jnp.float32),
        grid_spec=pltpu.PrefetchScalarGridSpec(
            num_scalar_prefetch=1,
            grid=(1024 // width,),
            in_specs=specs,
            out_specs=pl.BlockSpec((2, HALF, width), lambda n, s: (0, chunk, n)),
            scratch_shapes=[pltpu.VMEM((2 * HALF, 4096), jnp.bfloat16)],
        ),
        input_output_aliases=alias,
        compiler_params=pltpu.CompilerParams(vmem_limit_bytes=48 << 20),
        cost_estimate=pl.CostEstimate(flops=8 << 30, transcendentals=0, bytes_accessed=16 << 20),
    )(*args)


def form_body(place, *refs):
    blocks, z_ref, w_ref, out = refs[:8], refs[8], refs[9], refs[10]
    step = pl.program_id(0)

    @pl.when(step == 0)
    def _():
        out[...] = jnp.zeros_like(out)

    s_re = jnp.zeros((STEP, STEP), jnp.float32)
    s_im = jnp.zeros((STEP, STEP), jnp.float32)
    for i, block in enumerate(blocks):
        at = pl.multiple_of(place[i] * STEP, STEP)
        z_re, z_im = z_ref[0, :, pl.ds(at, STEP)], z_ref[1, :, pl.ds(at, STEP)]
        re, im = block[0].astype(jnp.float32), block[1].astype(jnp.float32)
        s_re += z_re * re - z_im * im
        s_im += z_re * im + z_im * re
    s_re = jnp.sum(s_re, axis=1, keepdims=True)
    s_im = jnp.sum(s_im, axis=1, keepdims=True)
    w_re, w_im = w_ref[0], w_ref[1]
    n = step // 2
    out[0, pl.ds(n, 1), :] += jnp.sum(w_re * s_re - w_im * s_im, axis=0, keepdims=True)
    out[1, pl.ds(n, 1), :] += jnp.sum(w_re * s_im + w_im * s_re, axis=0, keepdims=True)


def form(place, blocks, z, w):
    specs = [pl.BlockSpec((2, STEP, STEP), lambda i, s: (0, i, 0))] * 8
    specs.append(pl.BlockSpec((2, STEP, 1024), lambda i, s: (0, i, 0)))
    specs.append(pl.BlockSpec((2, STEP, 16), lambda i, s: (0, i, 0)))
    return pl.pallas_call(
        form_body,
        out_shape=jax.ShapeDtypeStruct((2, 4, 16), jnp.float32),
        grid_spec=pltpu.PrefetchScalarGridSpec(
            num_scalar_prefetch=1,
            grid=(8,),
            in_specs=specs,
            out_specs=pl.BlockSpec((2, 4, 16), lambda i, s: (0, 0, 0)),
        ),
        cost_estimate=pl.CostEstimate(flops=8 << 20, transcendentals=0, bytes_accessed=12 << 20),
    )(place, *blocks, z, w)


def local(screened, elements, energy_grid, band_index, energy_index):
    x_lo, y, z = lax.axis_index("x_lo"), lax.axis_index("y"), lax.axis_index("z")
    x_hi, core = lax.axis_index("x_hi"), lax.axis_index("core")
    w = weights(energy_grid, band_index, energy_index)

    turned = send(elements, TURN)
    across = send(elements, X_FAR)
    own = ring(elements, Z_UP, Z_DOWN, Z_ON, core) + ring(across, Z_UP, Z_DOWN, Z_ON, core)
    other = [send(block, CORE) for block in own]
    beside = send(turned, X_NEAR)
    columns = ring(turned, Y_UP, Y_DOWN, Y_ON, core) + ring(beside, Y_UP, Y_DOWN, Y_ON, core)

    back = jnp.array([0, 1, 3, 2], jnp.int32)
    layer = (z - back + 4) % 4
    chip = jnp.concatenate([layer * 2 + x_hi, layer * 2 + 1 - x_hi])
    row_place = jnp.concatenate([chip * 2 + core, chip * 2 + 1 - core])
    line = (y - back + 4) % 4
    source = jnp.concatenate([x_lo * 4 + line, (1 - x_lo) * 4 + line])
    taken = jnp.array(MATCH, jnp.int32)[(z * 2 + x_hi) * 2 + core]
    col_place = jnp.sum(jnp.where(source[:, None] == taken[None, :], jnp.arange(8, dtype=jnp.int32)[None, :], 0), axis=1)

    blocks = own + other
    zz = product(0, row_place, blocks, screened)
    zz = product(1, row_place, blocks, screened, zz)
    out = form(col_place, columns, zz, w)
    for pairs in ROUNDS:
        out = out + send(out, pairs)
    return out


def solution(mesh):
    split = Mesh(mesh.devices.reshape(2, 4, 4, 2, 2), AXES)
    in_specs = (P(None, ROW, COL), P(None, None, ROW + COL), P(), P(), P())
    return jax.shard_map(local, mesh=split, in_specs=in_specs, out_specs=P(), check_vma=False)
```

```python
import functools
import itertools

import jax
import jax.numpy as jnp
from jax import lax
from jax.experimental import pallas as pl
from jax.experimental.pallas import tpu as pltpu
from jax.sharding import Mesh
from jax.sharding import PartitionSpec as P

AXES = ("x_lo", "y", "z", "x_hi", "core")
ROW = ("x_lo", "y")
COL = ("z", "x_hi", "core")
STEP = 128
SCALE = 256 ** (-0.5)

MATCH = (
    (2, 0, 5, 7, 1, 3, 4, 6),
    (2, 3, 5, 4, 1, 0, 7, 6),
    (7, 4, 3, 1, 6, 5, 0, 2),
    (6, 7, 0, 2, 4, 5, 3, 1),
    (2, 0, 5, 4, 1, 3, 7, 6),
    (2, 0, 5, 4, 3, 1, 6, 7),
    (6, 4, 2, 1, 7, 5, 0, 3),
    (4, 6, 2, 0, 5, 7, 3, 1),
    (6, 4, 3, 1, 5, 7, 0, 2),
    (6, 7, 1, 0, 4, 5, 3, 2),
    (2, 0, 5, 6, 1, 3, 7, 4),
    (1, 3, 5, 4, 2, 0, 6, 7),
    (7, 6, 3, 1, 5, 4, 0, 2),
    (6, 7, 3, 1, 4, 5, 2, 0),
    (3, 0, 5, 7, 1, 2, 4, 6),
    (1, 3, 7, 5, 0, 2, 4, 6),
)


def pairs_of(move):
    found = []
    for x_lo, y, z, x_hi, core in itertools.product(range(2), range(4), range(4), range(2), range(2)):
        x, ny, nz, ncore = move(2 * x_hi + x_lo, y, z, core)
        x, ny, nz = x % 4, ny % 4, nz % 4
        source = (((x_lo * 4 + y) * 4 + z) * 2 + x_hi) * 2 + core
        found.append((source, (((x % 2 * 4 + ny) * 4 + nz) * 2 + x // 2) * 2 + ncore))
    return found


Z_ON = pairs_of(lambda x, y, z, c: (x, y, z + 1 - 2 * c, c))
Z_BACK = pairs_of(lambda x, y, z, c: (x, y, z - 1 + 2 * c, c))
Y_ON = pairs_of(lambda x, y, z, c: (x, y + 1 - 2 * c, z, c))
Y_FAR = pairs_of(lambda x, y, z, c: (x, y + 2, z, c))
Y_BACK = pairs_of(lambda x, y, z, c: (x, y - 1 + 2 * c, z, c))
X_FAR = pairs_of(lambda x, y, z, c: (x + 2, y, z, c))
X_NEAR = pairs_of(lambda x, y, z, c: (x ^ 1, y, z, c))
CORE = pairs_of(lambda x, y, z, c: (x, y, z, 1 - c))
TURN = [(c // 2 * 16 + c % 2 * 8 + j, MATCH[c][j] * 16 + c) for c in range(16) for j in range(8)]
ROUNDS = (
    CORE,
    X_NEAR,
    pairs_of(lambda x, y, z, c: (x + (1 if x % 2 else -1), y, z, c)),
    pairs_of(lambda x, y, z, c: (x, y ^ 1, z, c)),
    pairs_of(lambda x, y, z, c: (x, y + (1 if y % 2 else -1), z, c)),
    pairs_of(lambda x, y, z, c: (x, y, z ^ 1, c)),
    pairs_of(lambda x, y, z, c: (x, y, z + (1 if z % 2 else -1), c)),
)


def send(block, pairs):
    return lax.ppermute(block, AXES, pairs)


def after(value, *others):
    return lax.optimization_barrier((value, *others))[0]


def meet(*values):
    return lax.optimization_barrier(values)


def weights(energy_grid, band_index, energy_index):
    points = lax.broadcasted_iota(jnp.int32, (1, energy_grid.shape[0]), 1)
    band_energy = jnp.sum(
        jnp.where(band_index[:, None] == points, energy_grid[None, :], 0.0), axis=-1
    )
    eval_energy = jnp.sum(
        jnp.where(energy_index[:, :, None] == points[None], energy_grid[None, None, :], 0.0),
        axis=-1,
    )
    offset = eval_energy[:, None, :] - band_energy[None, :, None]
    denom = offset * offset + 0.25
    w = jnp.stack([offset / denom, -0.5 / denom])
    return w.reshape(2, -1, w.shape[-1])


VMEM = pl.BlockSpec(memory_space=pltpu.VMEM)


ANY = pl.BlockSpec(memory_space=pl.ANY)
HBM = pl.BlockSpec(memory_space=pltpu.HBM)


def keep_body(w_ref, out):
    out[...] = w_ref[...]


def keep(w):
    return pl.pallas_call(
        keep_body,
        out_shape=jax.ShapeDtypeStruct(w.shape, w.dtype),
        in_specs=[VMEM],
        out_specs=VMEM,
    )(w)


def product_body(first, pack, tags, *refs):
    refs = list(refs)
    blocks = [refs.pop(0) for _ in range(1 if "packed" in tags[-1] else len(tags))]
    if len(blocks) < len(tags):
        blocks = [blocks[0].at[i] for i in range(len(tags))]
    blocks = [block for block, tag in zip(blocks, tags, strict=True) if tag[2] != "skip"]
    tags = [tag for tag in tags if tag[2] != "skip"]
    count = len(tags)
    w_hbm = refs.pop(0)
    if not first:
        refs.pop(0)
    z_ref = refs.pop(0)
    out = refs.pop(0) if pack else None
    block_buf, w_buf, sems = refs
    z = lax.axis_index("z")
    copies = []
    for i, (past, back, other) in enumerate(tags):
        core, x_hi = lax.axis_index("core"), lax.axis_index("x_hi")
        core = 1 - core if other else core
        x_hi = 1 - x_hi if past else x_hi
        layer = (z + 4 - (1 - 2 * core) * back) & 3
        at = pl.multiple_of((layer * 4 + x_hi * 2 + core) * STEP, STEP)
        copies.append(pltpu.make_async_copy(blocks[i], block_buf.at[i], sems.at[0, i]))
        copies.append(pltpu.make_async_copy(w_hbm.at[:, pl.ds(at, STEP), :], w_buf.at[i], sems.at[1, i]))
    for copy in copies:
        copy.start()
    for some in (range(1), range(1, count)):
        for copy in copies[2 * some.start : 2 * some.stop]:
            copy.wait()
        if pack and some.start == 1:
            saved = pltpu.make_async_copy(block_buf, out, sems.at[2, 0])
            saved.start()
        w_re, w_im = [], []
        for i in some:
            x, y = w_buf[i, 0], w_buf[i, 1]
            w_re += [x, y]
            w_im += [y, -x]
        w_re, w_im = jnp.concatenate(w_re, axis=0), jnp.concatenate(w_im, axis=0)
        for m in range(2):
            at = pl.ds(m * 512, 512)
            lhs = jnp.concatenate([block_buf[i, part, at, :] for i in some for part in (0, 1)], axis=1)
            for part, w in ((0, w_re), (1, w_im)):
                value = jnp.dot(lhs, w, preferred_element_type=jnp.float32)
                if first and some.start == 0:
                    z_ref[part, at, :] = value
                else:
                    z_ref[part, at, :] += value
    if pack:
        saved.wait()


def product(tags, blocks, screened, z=None, pack=False):
    count = len(tags)
    args = [*blocks, screened]
    specs = [HBM] * len(args)
    shapes, outs = [jax.ShapeDtypeStruct((2, 1024, 1024), jnp.float32)], [VMEM]
    alias = {}
    if z is not None:
        args.append(z)
        specs.append(VMEM)
        alias = {len(args) - 1: 0}
    if pack:
        shapes.append(jax.ShapeDtypeStruct((count, 2, 1024, STEP), jnp.bfloat16))
        outs.append(HBM)
    return pl.pallas_call(
        functools.partial(product_body, z is None, pack, tags),
        out_shape=shapes,
        in_specs=specs,
        out_specs=outs,
        scratch_shapes=[
            pltpu.VMEM((count, 2, 1024, STEP), jnp.bfloat16),
            pltpu.VMEM((count, 2, STEP, 1024), jnp.bfloat16),
            pltpu.SemaphoreType.DMA((3, count)),
        ],
        input_output_aliases=alias,
        compiler_params=pltpu.CompilerParams(vmem_limit_bytes=40 << 20),
        cost_estimate=pl.CostEstimate(flops=1, transcendentals=0, bytes_accessed=1),
    )(*args)


def form_body(tags, *refs):
    count = len(tags)
    blocks, z_ref, w_ref, out = refs[:count], refs[count], refs[count + 1], refs[-1]
    group = (lax.axis_index("z") * 2 + lax.axis_index("x_hi")) * 2 + lax.axis_index("core")
    code = jnp.int32(0)
    for c in range(16):
        code = jnp.where(group == c, CODES[c], code)
    places = []
    for beside, back in tags:
        x_lo = lax.axis_index("x_lo")
        x_lo = 1 - x_lo if beside else x_lo
        way = 1 - 2 * lax.axis_index("core")
        source = x_lo * 4 + ((lax.axis_index("y") + 4 - way * back) & 3)
        places.append(pl.ds(pl.multiple_of(((code >> (3 * source)) & 7) * STEP, STEP), STEP))

    for n in range(4):
        o_re = jnp.zeros((1, 16), jnp.float32)
        o_im = jnp.zeros((1, 16), jnp.float32)
        for half in range(2):
            rows = pl.ds(n * 256 + half * STEP, STEP)
            s_re = jnp.zeros((STEP, STEP), jnp.float32)
            s_im = jnp.zeros((STEP, STEP), jnp.float32)
            for block, at in zip(blocks, places, strict=True):
                z_re, z_im = z_ref[0, rows, at], z_ref[1, rows, at]
                re, im = block[0, rows, :].astype(jnp.float32), block[1, rows, :].astype(jnp.float32)
                s_re += z_re * re - z_im * im
                s_im += z_re * im + z_im * re
            s_re = jnp.sum(s_re, axis=1, keepdims=True)
            s_im = jnp.sum(s_im, axis=1, keepdims=True)
            w_re, w_im = w_ref[0, rows, :], w_ref[1, rows, :]
            o_re += jnp.sum(w_re * s_re - w_im * s_im, axis=0, keepdims=True)
            o_im += jnp.sum(w_re * s_im + w_im * s_re, axis=0, keepdims=True)
        for part, o in ((0, o_re), (1, o_im)):
            o = o * SCALE
            if len(refs) > count + 3:
                o += refs[count + 2][part, n : n + 1, :]
            out[part, n : n + 1, :] = o


CODES = [sum(row.index(r) << (3 * r) for r in range(8)) for row in MATCH]


def form(tags, blocks, z, w, total=None):
    args = [*blocks, z, w] + ([] if total is None else [total])
    return pl.pallas_call(
        functools.partial(form_body, tags),
        out_shape=jax.ShapeDtypeStruct((2, 4, 16), jnp.float32),
        in_specs=[VMEM] * len(args),
        out_specs=VMEM,
        compiler_params=pltpu.CompilerParams(vmem_limit_bytes=8 << 20),
        cost_estimate=pl.CostEstimate(flops=1, transcendentals=0, bytes_accessed=1),
    )(*args)


def local(screened, elements, energy_grid, band_index, energy_index):
    w = keep(weights(energy_grid, band_index, energy_index))

    t0 = send(elements, TURN)
    p0 = send(elements, X_FAR)
    n1, n3 = send(elements, Z_ON), send(elements, Z_BACK)
    m0 = send(elements, CORE)
    n1, n3, w = meet(n1, n3, w)
    m1, m3, q0 = send(n1, CORE), send(n3, CORE), send(p0, CORE)
    t0, p0, n1, n3, m0, m1, m3, q0 = meet(t0, p0, n1, n3, m0, m1, m3, q0)

    t1, t3, t2 = send(t0, Y_ON), send(t0, Y_BACK), send(t0, Y_FAR)
    u0 = send(t0, X_NEAR)
    n2 = send(n1, Z_ON)
    z, = product(((0, 0, False), (0, 1, False), (0, 3, False), (1, 0, False)), [elements, n1, n3, p0], screened)
    p2 = send(n2, X_FAR)
    late = after(p0, n2)
    p1, p3 = send(late, Z_ON), send(late, Z_BACK)
    z, = product(((0, 0, True), (0, 1, True), (0, 3, True), (1, 0, True)), [m0, m1, m3, q0], screened, z)
    t1, t3, t2, u0, n2, p2, p1, p3, z = meet(t1, t3, t2, u0, n2, p2, p1, p3, z)

    u1, u3, u2 = send(u0, Y_ON), send(u0, Y_BACK), send(t2, X_NEAR)
    m2, q2, q1, q3 = [send(block, CORE) for block in (n2, p2, p1, p3)]
    z, = product(((0, 2, False), (1, 1, False), (1, 2, False), (1, 3, False)), [n2, p1, p2, p3], screened, z)
    z, = product(((0, 2, True), (1, 1, True), (1, 2, True), (1, 3, True)), [m2, q1, q2, q3], screened, z)
    tags = ((0, 0), (0, 1), (0, 2), (0, 3), (1, 0), (1, 1), (1, 3), (1, 2))
    out = form(tags, [t0, t1, t2, t3, u0, u1, u3, u2], z, w)
    for pairs in ROUNDS:
        out = out + send(out, pairs)
    return out


def solution(mesh):
    split = Mesh(mesh.devices.reshape(2, 4, 4, 2, 2), AXES)
    in_specs = (P(None, ROW, COL), P(None, None, ROW + COL), P(), P(), P())
    return jax.shard_map(local, mesh=split, in_specs=in_specs, out_specs=P(), check_vma=False)
```

```python
import functools
import itertools

import jax
import jax.numpy as jnp
from jax import lax
from jax.experimental import pallas as pl
from jax.experimental.pallas import tpu as pltpu
from jax.sharding import Mesh
from jax.sharding import PartitionSpec as P

AXES = ("x_lo", "y", "z", "x_hi", "core")
ROW = ("x_lo", "y")
COL = ("z", "x_hi", "core")
STEP = 128
SCALE = 256 ** (-0.5)

MATCH = (
    (2, 0, 5, 7, 1, 3, 4, 6),
    (2, 3, 5, 4, 1, 0, 7, 6),
    (7, 4, 3, 1, 6, 5, 0, 2),
    (6, 7, 0, 2, 4, 5, 3, 1),
    (2, 0, 5, 4, 1, 3, 7, 6),
    (2, 0, 5, 4, 3, 1, 6, 7),
    (6, 4, 2, 1, 7, 5, 0, 3),
    (4, 6, 2, 0, 5, 7, 3, 1),
    (6, 4, 3, 1, 5, 7, 0, 2),
    (6, 7, 1, 0, 4, 5, 3, 2),
    (2, 0, 5, 6, 1, 3, 7, 4),
    (1, 3, 5, 4, 2, 0, 6, 7),
    (7, 6, 3, 1, 5, 4, 0, 2),
    (6, 7, 3, 1, 4, 5, 2, 0),
    (3, 0, 5, 7, 1, 2, 4, 6),
    (1, 3, 7, 5, 0, 2, 4, 6),
)


def pairs_of(move):
    found = []
    for x_lo, y, z, x_hi, core in itertools.product(range(2), range(4), range(4), range(2), range(2)):
        x, ny, nz, ncore = move(2 * x_hi + x_lo, y, z, core)
        x, ny, nz = x % 4, ny % 4, nz % 4
        source = (((x_lo * 4 + y) * 4 + z) * 2 + x_hi) * 2 + core
        found.append((source, (((x % 2 * 4 + ny) * 4 + nz) * 2 + x // 2) * 2 + ncore))
    return found


Z_ON = pairs_of(lambda x, y, z, c: (x, y, z + 1 - 2 * c, c))
Z_BACK = pairs_of(lambda x, y, z, c: (x, y, z - 1 + 2 * c, c))
Y_ON = pairs_of(lambda x, y, z, c: (x, y + 1 - 2 * c, z, c))
Y_FAR = pairs_of(lambda x, y, z, c: (x, y + 2, z, c))
Y_BACK = pairs_of(lambda x, y, z, c: (x, y - 1 + 2 * c, z, c))
X_FAR = pairs_of(lambda x, y, z, c: (x + 2, y, z, c))
X_NEAR = pairs_of(lambda x, y, z, c: (x ^ 1, y, z, c))
CORE = pairs_of(lambda x, y, z, c: (x, y, z, 1 - c))
TURN = [(c // 2 * 16 + c % 2 * 8 + j, MATCH[c][j] * 16 + c) for c in range(16) for j in range(8)]
ROUNDS = (
    CORE,
    X_NEAR,
    pairs_of(lambda x, y, z, c: (x + (1 if x % 2 else -1), y, z, c)),
    pairs_of(lambda x, y, z, c: (x, y ^ 1, z, c)),
    pairs_of(lambda x, y, z, c: (x, y + (1 if y % 2 else -1), z, c)),
    pairs_of(lambda x, y, z, c: (x, y, z ^ 1, c)),
    pairs_of(lambda x, y, z, c: (x, y, z + (1 if z % 2 else -1), c)),
)


def send(block, pairs):
    return lax.ppermute(block, AXES, pairs)


def after(value, *others):
    return lax.optimization_barrier((value, *others))[0]


def meet(*values):
    return lax.optimization_barrier(values)


def weights(energy_grid, band_index, energy_index):
    points = lax.broadcasted_iota(jnp.int32, (1, energy_grid.shape[0]), 1)
    band_energy = jnp.sum(
        jnp.where(band_index[:, None] == points, energy_grid[None, :], 0.0), axis=-1
    )
    eval_energy = jnp.sum(
        jnp.where(energy_index[:, :, None] == points[None], energy_grid[None, None, :], 0.0),
        axis=-1,
    )
    offset = eval_energy[:, None, :] - band_energy[None, :, None]
    denom = offset * offset + 0.25
    w = jnp.stack([offset / denom, -0.5 / denom])
    return w.reshape(2, -1, w.shape[-1])


VMEM = pl.BlockSpec(memory_space=pltpu.VMEM)


ANY = pl.BlockSpec(memory_space=pl.ANY)
HBM = pl.BlockSpec(memory_space=pltpu.HBM)


def keep_body(w_ref, out):
    out[...] = w_ref[...]


def keep(w):
    return pl.pallas_call(
        keep_body,
        out_shape=jax.ShapeDtypeStruct(w.shape, w.dtype),
        in_specs=[VMEM],
        out_specs=VMEM,
    )(w)


def product_body(first, pack, tags, *refs):
    refs = list(refs)
    blocks = [refs.pop(0) for _ in range(1 if "packed" in tags[-1] else len(tags))]
    if len(blocks) < len(tags):
        blocks = [blocks[0].at[i] for i in range(len(tags))]
    blocks = [block for block, tag in zip(blocks, tags, strict=True) if tag[2] != "skip"]
    tags = [tag for tag in tags if tag[2] != "skip"]
    count = len(tags)
    w_hbm = refs.pop(0)
    if not first:
        refs.pop(0)
    z_ref = refs.pop(0)
    out = refs.pop(0) if pack else None
    block_buf, w_buf, sems = refs
    z = lax.axis_index("z")
    copies = []
    for i, (past, back, other) in enumerate(tags):
        core, x_hi = lax.axis_index("core"), lax.axis_index("x_hi")
        core = 1 - core if other else core
        x_hi = 1 - x_hi if past else x_hi
        layer = (z + 4 - (1 - 2 * core) * back) & 3
        at = pl.multiple_of((layer * 4 + x_hi * 2 + core) * STEP, STEP)
        copies.append(pltpu.make_async_copy(blocks[i], block_buf.at[i], sems.at[0, i]))
        copies.append(pltpu.make_async_copy(w_hbm.at[:, pl.ds(at, STEP), :], w_buf.at[i], sems.at[1, i]))
    for copy in copies:
        copy.start()
    for some in (range(1), range(1, count)):
        for copy in copies[2 * some.start : 2 * some.stop]:
            copy.wait()
        if pack and some.start == 1:
            saved = pltpu.make_async_copy(block_buf, out, sems.at[2, 0])
            saved.start()
        w_re, w_im = [], []
        for i in some:
            x, y = w_buf[i, 0], w_buf[i, 1]
            w_re += [x, y]
            w_im += [y, -x]
        w_re, w_im = jnp.concatenate(w_re, axis=0), jnp.concatenate(w_im, axis=0)
        for m in range(2):
            at = pl.ds(m * 512, 512)
            lhs = jnp.concatenate([block_buf[i, part, at, :] for i in some for part in (0, 1)], axis=1)
            for part, w in ((0, w_re), (1, w_im)):
                value = jnp.dot(lhs, w, preferred_element_type=jnp.float32)
                if first and some.start == 0:
                    z_ref[part, at, :] = value
                else:
                    z_ref[part, at, :] += value
    if pack:
        saved.wait()


def product(tags, blocks, screened, z=None, pack=False):
    count = len(tags)
    args = [*blocks, screened]
    specs = [HBM] * len(args)
    shapes, outs = [jax.ShapeDtypeStruct((2, 1024, 1024), jnp.float32)], [VMEM]
    alias = {}
    if z is not None:
        args.append(z)
        specs.append(VMEM)
        alias = {len(args) - 1: 0}
    if pack:
        shapes.append(jax.ShapeDtypeStruct((count, 2, 1024, STEP), jnp.bfloat16))
        outs.append(HBM)
    return pl.pallas_call(
        functools.partial(product_body, z is None, pack, tags),
        out_shape=shapes,
        in_specs=specs,
        out_specs=outs,
        scratch_shapes=[
            pltpu.VMEM((count, 2, 1024, STEP), jnp.bfloat16),
            pltpu.VMEM((count, 2, STEP, 1024), jnp.bfloat16),
            pltpu.SemaphoreType.DMA((3, count)),
        ],
        input_output_aliases=alias,
        compiler_params=pltpu.CompilerParams(vmem_limit_bytes=40 << 20),
        cost_estimate=pl.CostEstimate(flops=1, transcendentals=0, bytes_accessed=1),
    )(*args)


def form_body(tags, *refs):
    count = len(tags)
    blocks, z_ref, w_ref, out = refs[:count], refs[count], refs[count + 1], refs[-1]
    group = (lax.axis_index("z") * 2 + lax.axis_index("x_hi")) * 2 + lax.axis_index("core")
    code = jnp.int32(0)
    for c in range(16):
        code = jnp.where(group == c, CODES[c], code)
    places = []
    for beside, back in tags:
        x_lo = lax.axis_index("x_lo")
        x_lo = 1 - x_lo if beside else x_lo
        way = 1 - 2 * lax.axis_index("core")
        source = x_lo * 4 + ((lax.axis_index("y") + 4 - way * back) & 3)
        places.append(pl.ds(pl.multiple_of(((code >> (3 * source)) & 7) * STEP, STEP), STEP))

    for n in range(4):
        o_re = jnp.zeros((1, 16), jnp.float32)
        o_im = jnp.zeros((1, 16), jnp.float32)
        for half in range(2):
            rows = pl.ds(n * 256 + half * STEP, STEP)
            s_re = jnp.zeros((STEP, STEP), jnp.float32)
            s_im = jnp.zeros((STEP, STEP), jnp.float32)
            for block, at in zip(blocks, places, strict=True):
                z_re, z_im = z_ref[0, rows, at], z_ref[1, rows, at]
                re, im = block[0, rows, :].astype(jnp.float32), block[1, rows, :].astype(jnp.float32)
                s_re += z_re * re - z_im * im
                s_im += z_re * im + z_im * re
            s_re = jnp.sum(s_re, axis=1, keepdims=True)
            s_im = jnp.sum(s_im, axis=1, keepdims=True)
            w_re, w_im = w_ref[0, rows, :], w_ref[1, rows, :]
            o_re += jnp.sum(w_re * s_re - w_im * s_im, axis=0, keepdims=True)
            o_im += jnp.sum(w_re * s_im + w_im * s_re, axis=0, keepdims=True)
        for part, o in ((0, o_re), (1, o_im)):
            o = o * SCALE
            if len(refs) > count + 3:
                o += refs[count + 2][part, n : n + 1, :]
            out[part, n : n + 1, :] = o


CODES = [sum(row.index(r) << (3 * r) for r in range(8)) for row in MATCH]


def form(tags, blocks, z, w, total=None):
    args = [*blocks, z, w] + ([] if total is None else [total])
    return pl.pallas_call(
        functools.partial(form_body, tags),
        out_shape=jax.ShapeDtypeStruct((2, 4, 16), jnp.float32),
        in_specs=[VMEM] * len(args),
        out_specs=VMEM,
        compiler_params=pltpu.CompilerParams(vmem_limit_bytes=8 << 20),
        cost_estimate=pl.CostEstimate(flops=1, transcendentals=0, bytes_accessed=1),
    )(*args)


def local(screened, elements, energy_grid, band_index, energy_index):
    w = keep(weights(energy_grid, band_index, energy_index))

    t0 = send(elements, TURN)
    p0 = send(elements, X_FAR)
    n1, n3 = send(elements, Z_ON), send(elements, Z_BACK)
    m0 = send(elements, CORE)
    n1, n3, w = meet(n1, n3, w)
    m1, m3, q0 = send(n1, CORE), send(n3, CORE), send(p0, CORE)
    t0, p0, n1, n3, m0, m1, m3, q0 = meet(t0, p0, n1, n3, m0, m1, m3, q0)

    t1, t3, t2 = send(t0, Y_ON), send(t0, Y_BACK), send(t0, Y_FAR)
    u0 = send(t0, X_NEAR)
    n2 = send(n1, Z_ON)
    z, = product(((0, 0, False), (0, 1, False), (0, 3, False), (1, 0, False)), [elements, n1, n3, p0], screened)
    p2 = send(after(n2, z), X_FAR)
    late = after(p0, n2)
    p1, p3 = send(late, Z_ON), send(late, Z_BACK)
    z, = product(((0, 0, True), (0, 1, True), (0, 3, True), (1, 0, True)), [m0, m1, m3, q0], screened, z)
    t1, t3, t2, u0 = meet(t1, t3, t2, u0)

    u1, u3, u2 = send(u0, Y_ON), send(u0, Y_BACK), send(t2, X_NEAR)
    m2, q2, q1, q3 = [send(block, CORE) for block in (n2, p2, p1, p3)]
    z, = product(((0, 2, False), (1, 1, False), (1, 2, False), (1, 3, False)), [n2, p1, p2, p3], screened, z)
    z, = product(((0, 2, True), (1, 1, True), (1, 2, True), (1, 3, True)), [m2, q1, q2, q3], screened, z)
    tags = ((0, 0), (0, 1), (0, 2), (0, 3), (1, 0), (1, 1), (1, 3), (1, 2))
    out = form(tags, [t0, t1, t2, t3, u0, u1, u3, u2], z, w)
    for pairs in ROUNDS:
        out = out + send(out, pairs)
    return out


def solution(mesh):
    split = Mesh(mesh.devices.reshape(2, 4, 4, 2, 2), AXES)
    in_specs = (P(None, ROW, COL), P(None, None, ROW + COL), P(), P(), P())
    return jax.shard_map(local, mesh=split, in_specs=in_specs, out_specs=P(), check_vma=False)
```
